32 devices in a mesh: dp: 8 (over y, x, core), mp: 4 (over z).
Axes of the slice: x: 2, y: 2, z: 4, core: 2. Of those that a mesh axis runs over, the one named last changes fastest.
Arguments:
- tokens: bfloat16 [2, 1024, 4096], P(None, 'dp', 'mp'), may hold values from -6 to 6
- targets: bfloat16 [2, 1024, 4096], P(None, 'dp', 'mp'), may hold values from -6 to 6
- weight: bfloat16 [4096, 4096], P('mp'), may hold values from -0.09375 to 0.09375
- basis: bfloat16 [4096, 512], replicated, may hold values from -0.09375 to 0.09375
- moment1: float32 [4, 1024, 512], P('mp', 'dp'), may hold values from -0.06 to 0.06
- moment2: float32 [4, 1024, 512], P('mp', 'dp'), may hold values from 1e-05 to 0.001
Outputs:
- new_weight: bfloat16 [4096, 4096], P('mp')
- new_moment1: float32 [4, 1024, 512], P('mp', 'dp')
- new_moment2: float32 [4, 1024, 512], P('mp', 'dp')
The draws below stay inside these ranges and needn't reach their ends.
All inputs are finite; a program needn't handle non-finite values.
Results may differ from the reference program's by a relative error of at most 0.009.
Values may be sent and summed in bfloat16 or wider, within the bound.
A program may use at most 64 MiB of HBM per device.

```python
import math
import jax
import jax.numpy as jnp
from jax import lax

D_OUT = 4096
D_IN = 4096
RANK = 512
TOKENS = 1024
ROWS_MP = 1024
N_MP = 4


def block_scale(key, extent, shards, least, top_value):
    def one(axis_at, parts):
        heights = jax.random.uniform(jax.random.fold_in(jax.random.fold_in(key, 6), axis_at), (parts,), jnp.float32, least / len(shards), top_value / len(shards))
        return jnp.repeat(jnp.exp(heights), extent[axis_at] // parts).reshape((-1,) + (1,) * (len(extent) - axis_at - 1))

    loudness = one(*shards[0])
    for cut in shards[1:]:
        loudness = loudness * one(*cut)
    return loudness


def scatter_about(key, dims, deviation, bound, pieces=(), held_as=jnp.bfloat16):
    result = jax.random.normal(key, dims, jnp.float32) * deviation
    if len(pieces) > 0:
        result = block_scale(key, dims, pieces, -0.22, 0.18) * result
    return jnp.clip(result, min=-bound, max=bound).astype(held_as)


def setup_inputs(seed: int = 0) -> dict:
    arg_keys = jax.random.split(jax.random.key(seed), 7)
    return {
        "tokens": scatter_about(arg_keys[0], (2, TOKENS, D_IN), 1.0, 6.0, ((1, 8), (2, 4))),
        "targets": scatter_about(arg_keys[1], (2, TOKENS, D_OUT), 1.0, 6.0, ((1, 8), (2, 4))),
        "weight": scatter_about(arg_keys[2], (D_OUT, D_IN), D_IN ** -0.5, 0.09375, ((0, 4),)),
        "basis": scatter_about(arg_keys[3], (D_IN, RANK), D_IN ** -0.5, 0.09375),
        "moment1": scatter_about(arg_keys[4], (N_MP, ROWS_MP, RANK), 0.01, 0.06, ((0, 4), (1, 8)), jnp.float32),
        "moment2": jnp.clip(jnp.exp(math.log(0.001) - 4.6051703 * jax.random.uniform(arg_keys[5], (N_MP, ROWS_MP, RANK), jnp.float32) ** block_scale(arg_keys[5], (N_MP, ROWS_MP, RANK), ((0, 4), (1, 8)), -0.2, 0.2)), 9.999999747378752e-06, 0.001),
    }


def reference(tokens, targets, weight, basis, moment1, moment2):
    first = moment1.reshape(D_OUT, RANK)
    second = moment2.reshape(D_OUT, RANK)
    current = weight
    for turn in range(2):
        inputs = tokens[turn]
        outputs = jnp.dot(inputs, current.T, preferred_element_type=jnp.float32).astype(jnp.bfloat16)
        errors = (outputs.astype(jnp.float32) - targets[turn].astype(jnp.float32)).astype(jnp.bfloat16)
        reduced = jnp.dot(inputs, basis, preferred_element_type=jnp.float32)
        projected = jnp.dot(errors.astype(jnp.float32).T, reduced, precision=lax.Precision.HIGHEST) / TOKENS
        first = 0.9 * first + 0.1 * projected
        second = 0.95 * second + 0.05 * projected * projected
        direction = (first / (jnp.sqrt(second) + 1e-08)).astype(jnp.bfloat16)
        lifted = jnp.dot(direction, basis.T, preferred_element_type=jnp.float32)
        current = (current.astype(jnp.float32) - 0.02 * lifted).astype(jnp.bfloat16)
    return (current, first.reshape(N_MP, ROWS_MP, RANK), second.reshape(N_MP, ROWS_MP, RANK))
```

```python
import functools

import jax
import jax.numpy as jnp
from jax import lax
from jax.experimental import pallas as pl
from jax.experimental.pallas import tpu as pltpu
from jax.sharding import PartitionSpec as P

F32 = jnp.float32
BF16 = jnp.bfloat16


def dot_nt(a, b):
    return lax.dot_general(a, b, (((1,), (1,)), ((), ())), preferred_element_type=F32)


def dot_tn(a, b):
    return lax.dot_general(a, b, (((0,), (0,)), ((), ())), preferred_element_type=F32)


def kernel(
    n_dp, n_mp, total_tokens,
    tok, tgt_hbm, w_hbm, b_hbm, m_hbm, v_hbm,
    d_out, m_out, v_out,
    xbuf, tgt, w, b, mom1, mom2, y, r, g, send1, recv1, send2, recv2, dall,
    l_sem, x_send, x_recv, s1_send, s1_recv, s2_send, s2_recv, d_send, d_recv, o_sem,
):
    dp = lax.axis_index("dp")
    mp = lax.axis_index("mp")
    core = lax.rem(dp, 2)
    chip = lax.div(dp, 2)
    partner = dp + 1 - 2 * core
    n_ch = n_dp // 2
    out_rows, features = w_hbm.shape
    rows = out_rows // n_dp
    fin = features // n_mp
    tile = min(512, out_rows)
    tiles = out_rows // tile

    def mp_at(k):
        return lax.rem(mp + k, n_mp)

    def chip_at(k):
        return lax.rem(chip + k, n_ch)

    def columns(j):
        return pl.ds(pl.multiple_of(j * fin, fin), fin)

    def owner_rows(i):
        return pl.ds(pl.multiple_of(i * rows, rows), rows)

    def remote(src, dst, send, recv, where):
        return pltpu.make_async_remote_copy(
            src_ref=src, dst_ref=dst, send_sem=send, recv_sem=recv,
            device_id=where, device_id_type=pl.DeviceIdType.MESH,
        )

    k_copy = pltpu.make_async_copy(tok, xbuf.at[:, mp], l_sem.at[n_mp + 4])
    k_copy.start()

    barrier = pltpu.get_barrier_semaphore()
    peers = [(dp, mp_at(k)) for k in range(1, n_mp)]
    peers += [(chip_at(k) * 2 + core, mp) for k in range(1, n_ch)]
    peers += [(partner, mp)]
    for peer in peers:
        pl.semaphore_signal(barrier, inc=1, device_id=peer, device_id_type=pl.DeviceIdType.MESH)

    b_copy = pltpu.make_async_copy(b_hbm, b, l_sem.at[n_mp])
    t_copy = pltpu.make_async_copy(tgt_hbm, tgt, l_sem.at[n_mp + 1])
    m_copy = pltpu.make_async_copy(m_hbm.at[0], mom1, l_sem.at[n_mp + 2])
    v_copy = pltpu.make_async_copy(v_hbm.at[0], mom2, l_sem.at[n_mp + 3])
    w_copies = []
    for k in range(n_mp):
        j = mp_at(k)
        w_copies.append(pltpu.make_async_copy(w_hbm.at[:, columns(j)], w.at[j], l_sem.at[k]))
    b_copy.start()
    for copy in w_copies:
        copy.start()
    t_copy.start()
    m_copy.start()
    v_copy.start()

    k_copy.wait()
    pl.semaphore_wait(barrier, len(peers))

    low = (mp < n_mp // 2).astype(jnp.int32)

    def other_at(i):
        down = n_mp - 1 - i
        down = down - (down <= mp).astype(jnp.int32)
        up = i + (mp <= i).astype(jnp.int32)
        return low * down + (1 - low) * up

    def token_copy(s, j, lane, where):
        part = xbuf.at[s, j]
        return remote(part, part, x_send.at[s, lane], x_recv.at[s, j], (dp, where))

    def own_send(s):
        for lane, (onward, to) in enumerate(((mp > 0, mp - 1), (mp < n_mp - 1, mp + 1))):
            pl.when(onward)(token_copy(s, mp, lane, to).start)

    def own_sent(s):
        for lane, (onward, to) in enumerate(((mp > 0, mp - 1), (mp < n_mp - 1, mp + 1))):
            pl.when(onward)(token_copy(s, mp, lane, to).wait_send)

    def hop(s, i):
        j = other_at(i)
        below = (j > mp).astype(jnp.int32)
        to = mp + 1 - 2 * below
        onward = jnp.logical_and(to >= 0, to < n_mp)
        return onward, token_copy(s, j, 2 + i, to)

    def forward(s, i):
        onward, copy = hop(s, i)
        copy.wait_recv()
        pl.when(onward)(copy.start)

    def forwarded(s, i):
        onward, copy = hop(s, i)
        pl.when(onward)(copy.wait_send)

    def block(s, j, first):
        x = xbuf[s, j]
        for i in range(tiles):
            at = slice(i * tile, (i + 1) * tile)
            term = dot_nt(x, w[j, at, :])
            if first:
                y[s, :, at] = term
            else:
                y[s, :, at] += term
        term = jnp.dot(x, b[columns(j), :], preferred_element_type=F32)
        if first:
            r[s] = term
        else:
            r[s] += term

    def arrive(s, i):
        forward(s, i)
        block(s, other_at(i), False)

    sends = []

    def gradient(s):
        reduced = r[s].astype(BF16)
        for i in range(tiles):
            at = slice(i * tile, (i + 1) * tile)
            outputs = y[s, :, at]
            if s == 1:
                outputs = outputs + dot_nt(reduced, dall[at, :])
            outputs = outputs.astype(BF16).astype(F32)
            e = (outputs - tgt[s, :, at].astype(F32)).astype(BF16)
            g[at, :] = dot_tn(e, reduced)

    def swap(s, c):
        return remote(
            send1.at[s, c], recv1.at[s, c], s1_send.at[s, c], s1_recv.at[s, c], (partner, mp)
        )

    def swap_start(s):
        for k in range(1, n_ch + 1):
            c = chip_at(k)
            send1[s, c] = g[owner_rows(c * 2 + 1 - core), :].astype(BF16)
            copy = swap(s, c)
            copy.start()
            sends.append(copy)

    def scatter_start(s):
        for k in range(1, n_ch + 1):
            c = chip_at(k)
            swap(s, c).wait_recv()
            total = g[owner_rows(c * 2 + core), :] + recv1[s, c].astype(F32)
            if k < n_ch:
                send2[s, c] = total.astype(BF16)
                out = remote(
                    send2.at[s, c], recv2.at[s, chip], s2_send.at[s, c], s2_recv.at[s, chip],
                    (c * 2 + core, mp),
                )
                out.start()
                sends.append(out)
            else:
                g[owner_rows(c * 2 + core), :] = total

    def scatter_finish(s):
        total = g[owner_rows(dp), :]
        for k in range(1, n_ch):
            c = chip_at(k)
            remote(
                send2.at[s, c], recv2.at[s, c], s2_send.at[s, c], s2_recv.at[s, c],
                (c * 2 + core, mp),
            ).wait_recv()
            total = total + recv2[s, c].astype(F32)
        projected = total / total_tokens
        first = 0.9 * mom1[...] + 0.1 * projected
        second = 0.95 * mom2[...] + 0.05 * projected * projected
        mom1[...] = first
        mom2[...] = second
        step = (-0.02) * (first / (jnp.sqrt(second) + 1e-08))
        if s == 0:
            dall[owner_rows(dp), :] = step.astype(BF16)
        else:
            d_out[owner_rows(dp), :] = (dall[owner_rows(dp), :].astype(F32) + step).astype(BF16)

    def direction_copy(s, owner, sem_at, where):
        part = (d_out if s else dall).at[owner_rows(owner), :]
        return remote(part, part, d_send.at[s, sem_at], d_recv.at[s, owner], where)

    def gather_start(s):
        for k in range(1, n_ch):
            c = chip_at(k)
            copy = direction_copy(s, dp, c, (c * 2 + core, mp))
            copy.start()
            sends.append(copy)
        copy = direction_copy(s, dp, n_ch + chip, (partner, mp))
        copy.start()
        sends.append(copy)

    def gather_forward(s):
        for k in range(1, n_ch):
            c = chip_at(k)
            owner = c * 2 + core
            direction_copy(s, owner, c, (owner, mp)).wait_recv()
            copy = direction_copy(s, owner, n_ch + c, (partner, mp))
            copy.start()
            sends.append(copy)

    def gather_finish(s):
        for k in range(n_ch):
            c = chip_at(k)
            direction_copy(s, c * 2 + 1 - core, n_ch + c, (partner, mp)).wait_recv()

    last = n_mp - 2
    own_send(0)
    b_copy.wait()
    for copy in w_copies:
        copy.wait()
    block(0, mp, True)
    for k in range(n_mp - 1):
        i = n_mp - 2 - k
        forward(0, i)
        if k == 0:
            own_send(1)
        block(0, other_at(i), False)
    t_copy.wait()
    m_copy.wait()
    v_copy.wait()
    gradient(0)
    swap_start(0)
    block(1, mp, True)
    scatter_start(0)
    for k in range(n_mp - 2):
        arrive(1, n_mp - 2 - k)
    inner = jnp.logical_and(mp > 0, mp < n_mp - 1)
    pl.when(inner)(lambda: forward(1, 0))
    scatter_finish(0)
    gather_start(0)
    gather_forward(0)
    pl.when(jnp.logical_not(inner))(lambda: forward(1, 0))
    block(1, other_at(0), False)
    gather_finish(0)
    gradient(1)
    swap_start(1)
    scatter_start(1)
    scatter_finish(1)
    gather_start(1)
    m_done = pltpu.make_async_copy(mom1, m_out.at[0], o_sem.at[0])
    v_done = pltpu.make_async_copy(mom2, v_out.at[0], o_sem.at[1])
    m_done.start()
    v_done.start()
    gather_forward(1)
    gather_finish(1)
    for copy in sends:
        copy.wait_send()
    for s in (0, 1):
        own_sent(s)
        for i in range(n_mp - 1):
            forwarded(s, i)
    m_done.wait()
    v_done.wait()


def last_lift(width, w, d, b, first, second, w_out, m_out, v_out, stage, sem, s_sem):
    m_copy = pltpu.make_async_copy(first, m_out, s_sem.at[0])
    v_copy = pltpu.make_async_copy(second, v_out, s_sem.at[1])
    m_copy.start()
    v_copy.start()
    copies = []
    for i in range(w.shape[1] // width):
        at = slice(i * width, (i + 1) * width)
        stage[:, at] = (w[:, at].astype(F32) + dot_nt(d[...], b[at, :])).astype(BF16)
        copy = pltpu.make_async_copy(stage.at[:, at], w_out.at[:, at], sem.at[i])
        copy.start()
        copies.append(copy)
    for copy in copies:
        copy.wait()
    m_copy.wait()
    v_copy.wait()


def local(n_dp, n_mp, tokens, targets, weight, basis, moment1, moment2):
    steps, toks, fin = tokens.shape
    out_rows, features = weight.shape
    rank = basis.shape[1]
    rows = moment1.shape[1]
    n_ch = n_dp // 2
    hbm = pl.BlockSpec(memory_space=pltpu.HBM)
    vmem = pl.BlockSpec(memory_space=pltpu.VMEM)
    anywhere = pl.BlockSpec(memory_space=pl.ANY)
    dma = pltpu.SemaphoreType.DMA
    d, first, second = pl.pallas_call(
        functools.partial(kernel, n_dp, n_mp, toks * n_dp),
        out_shape=(
            jax.ShapeDtypeStruct((out_rows, rank), BF16),
            jax.ShapeDtypeStruct((1, rows, rank), F32),
            jax.ShapeDtypeStruct((1, rows, rank), F32),
        ),
        in_specs=[hbm] * 6,
        out_specs=(vmem, anywhere, anywhere),
        scratch_shapes=[
            pltpu.VMEM((steps, n_mp, toks, fin), BF16),
            pltpu.VMEM((steps, toks, out_rows), BF16),
            pltpu.VMEM((n_mp, out_rows, fin), BF16),
            pltpu.VMEM((features, rank), BF16),
            pltpu.VMEM((rows, rank), F32),
            pltpu.VMEM((rows, rank), F32),
            pltpu.VMEM((steps, toks, out_rows), F32),
            pltpu.VMEM((steps, toks, rank), F32),
            pltpu.VMEM((out_rows, rank), F32),
            pltpu.VMEM((steps, n_ch, rows, rank), BF16),
            pltpu.VMEM((steps, n_ch, rows, rank), BF16),
            pltpu.VMEM((steps, n_ch, rows, rank), BF16),
            pltpu.VMEM((steps, n_ch, rows, rank), BF16),
            pltpu.VMEM((out_rows, rank), BF16),
            dma((n_mp + 5,)),
            dma((steps, n_mp + 1)),
            dma((steps, n_mp)),
            dma((steps, n_ch)),
            dma((steps, n_ch)),
            dma((steps, n_ch)),
            dma((steps, n_ch)),
            dma((steps, n_dp)),
            dma((steps, n_dp)),
            dma((2,)),
        ],
        compiler_params=pltpu.CompilerParams(
            collective_id=0, has_side_effects=True, vmem_limit_bytes=30 * 2**20
        ),
    )(*[
        pltpu.with_memory_space_constraint(x, pltpu.HBM)
        for x in (tokens, targets, weight, basis, moment1, moment2)
    ])
    width = min(512, features)
    return pl.pallas_call(
        functools.partial(last_lift, width),
        out_shape=(
            jax.ShapeDtypeStruct((out_rows, features), BF16),
            jax.ShapeDtypeStruct((1, rows, rank), F32),
            jax.ShapeDtypeStruct((1, rows, rank), F32),
        ),
        in_specs=[vmem] * 5,
        out_specs=(hbm,) * 3,
        scratch_shapes=[
            pltpu.VMEM((out_rows, features), BF16), dma((features // width,)), dma((2,))
        ],
        compiler_params=pltpu.CompilerParams(vmem_limit_bytes=12 * 2**20),
    )(weight, d, basis, first, second)


def solution(mesh):
    in_specs = (
        P(None, "dp", "mp"),
        P(None, "dp", "mp"),
        P("mp", None),
        P(),
        P("mp", "dp", None),
        P("mp", "dp", None),
    )
    out_specs = (P("mp", None), P("mp", "dp", None), P("mp", "dp", None))
    body = functools.partial(local, mesh.shape["dp"], mesh.shape["mp"])
    return jax.shard_map(body, mesh=mesh, in_specs=in_specs, out_specs=out_specs, check_vma=False)
```

```python
import functools

import jax
import jax.numpy as jnp
from jax import lax
from jax.experimental import pallas as pl
from jax.experimental.pallas import tpu as pltpu
from jax.sharding import PartitionSpec as P

F32 = jnp.float32
BF16 = jnp.bfloat16


def dot_nt(a, b):
    return lax.dot_general(a, b, (((1,), (1,)), ((), ())), preferred_element_type=F32)


def dot_tn(a, b):
    return lax.dot_general(a, b, (((0,), (0,)), ((), ())), preferred_element_type=F32)


def kernel(
    n_dp, n_mp, total_tokens,
    tok, tgt_hbm, w_hbm, b_hbm, m_hbm, v_hbm,
    w_out, d_out, m_out, v_out,
    xbuf, x1, tgt, w, b, mom1, mom2, y, r, g, send1, recv1, send2, recv2,
    rall, rpart, zsend, zrecv, cpad, d0, corr,
    l_sem, x_send, x_recv, c_send, c_recv, z_send, z_recv,
    s1_send, s1_recv, s2_send, s2_recv, d_send, d_recv, o_sem,
):
    dp = lax.axis_index("dp")
    mp = lax.axis_index("mp")
    core = lax.rem(dp, 2)
    chip = lax.div(dp, 2)
    side = lax.rem(chip, 2)
    pair = lax.div(chip, 2)
    partner = dp + 1 - 2 * core
    n_ch = n_dp // 2
    n_pairs = n_ch // 2
    toks = x1.shape[0]
    out_rows, features = w_hbm.shape
    rows = out_rows // n_dp
    fin = features // n_mp
    piece = toks // n_mp
    chunk = fin // n_dp
    window = cpad.shape[1]
    start = lax.div(dp * chunk, window) * window
    inside = dp * chunk - start
    tile = min(512, out_rows)
    tiles = out_rows // tile
    per_tile = tile // (2 * rows)
    inner = jnp.logical_and(mp > 0, mp < n_mp - 1)
    outer = jnp.logical_not(inner)

    def mp_at(k):
        return lax.rem(mp + k, n_mp)

    near = pair * 2 + 1 - side
    others = []
    for k in range(1, n_pairs):
        q = lax.rem(pair + k, n_pairs)
        others += [q * 2 + 1 - side, q * 2 + side]
    others.append(near)

    def block_at(i, size):
        return pl.ds(pl.multiple_of(i * size, size), size)

    def columns(j):
        return block_at(j, fin)

    def owner_rows(i):
        return block_at(i, rows)

    def remote(src, dst, send, recv, where):
        return pltpu.make_async_remote_copy(
            src_ref=src, dst_ref=dst, send_sem=send, recv_sem=recv,
            device_id=where, device_id_type=pl.DeviceIdType.MESH,
        )

    loads = iter(range(l_sem.shape[0]))

    def load(src, dst):
        copy = pltpu.make_async_copy(src, dst, l_sem.at[next(loads)])
        copy.start()
        return copy

    x1_copy = load(tok.at[1], x1)
    b_copies = [load(b_hbm.at[columns(mp)], b.at[columns(mp)])]
    x0_copy = load(tok.at[0], xbuf.at[mp])

    barrier = pltpu.get_barrier_semaphore()
    peers = [(dp, mp_at(k)) for k in range(1, n_mp)]
    peers += [(c * 2 + core, mp) for c in others]
    peers += [(partner, mp)]
    for peer in peers:
        pl.semaphore_signal(barrier, inc=1, device_id=peer, device_id_type=pl.DeviceIdType.MESH)

    for k in range(1, n_mp):
        b_copies.append(load(b_hbm.at[columns(mp_at(k))], b.at[columns(mp_at(k))]))
    w_copies = [load(w_hbm.at[:, columns(mp_at(k))], w.at[mp_at(k)]) for k in range(n_mp)]
    t_copy = load(tgt_hbm, tgt)
    m_copy = load(m_hbm.at[0], mom1)
    v_copy = load(v_hbm.at[0], mom2)
    sends = []

    def go(copy):
        copy.start()
        sends.append(copy)

    low = (mp < n_mp // 2).astype(jnp.int32)

    def other_at(i):
        down = n_mp - 1 - i
        down = down - (down <= mp).astype(jnp.int32)
        up = i + (mp <= i).astype(jnp.int32)
        return low * down + (1 - low) * up

    order = list(reversed(range(n_mp - 1)))

    class Relay:
        def __init__(self, at, parts, send, recv):
            self.at, self.parts, self.send, self.recv = at, parts, send, recv
            self.hops = [(i, c) for c in range(parts) for i in order[:2]]
            self.hops += [(i, c) for i in order[2:] for c in range(parts)]

        def copy(self, j, lane, c, where):
            part = self.at(j, c)
            return remote(part, part, self.send.at[lane, c], self.recv.at[j, c], (dp, where))

        def own(self, act):
            for c in range(self.parts):
                for lane, (onward, to) in enumerate(((mp > 0, mp - 1), (mp < n_mp - 1, mp + 1))):
                    copy = self.copy(mp, lane, c, to)
                    pl.when(onward)(copy.start if act else copy.wait_send)

        def hop(self, i, c):
            j = other_at(i)
            below = (j > mp).astype(jnp.int32)
            to = mp + 1 - 2 * below
            onward = jnp.logical_and(to >= 0, to < n_mp)
            return onward, self.copy(j, 2 + i, c, to)

        def forward(self, hops):
            for i, c in hops:
                onward, copy = self.hop(i, c)
                copy.wait_recv()
                pl.when(onward)(copy.start)

        def pull(self, i):
            self.forward([(i, c) for c in range(self.parts)])

        def sent(self):
            self.own(False)
            for i, c in self.hops:
                onward, copy = self.hop(i, c)
                pl.when(onward)(copy.wait_send)

    half = toks // 2
    xs = Relay(lambda j, c: xbuf.at[j, c * half:(c + 1) * half], 2, x_send, x_recv)
    c_parts = 2 if chunk % 32 == 0 else 1
    c_size = chunk // c_parts
    cs = Relay(
        lambda j, c: cpad.at[j, pl.ds(pl.multiple_of(inside + c * c_size, c_size), c_size)],
        c_parts, c_send, c_recv,
    )

    def block(j, first):
        x = xbuf[j]
        for i in range(tiles):
            at = slice(i * tile, (i + 1) * tile)
            term = dot_nt(x, w[j, at, :])
            if first:
                y[:, at] = term
            else:
                y[:, at] += term
        term = jnp.dot(x, b[columns(j), :], preferred_element_type=F32)
        if first:
            r[...] = term
        else:
            r[...] += term

    def swap(s, c):
        return remote(
            send1.at[s, c], recv1.at[s, c], s1_send.at[s, c], s1_recv.at[s, c], (partner, mp)
        )

    def swap_start(s, i):
        for c in range(i * per_tile, (i + 1) * per_tile):
            send1[s, c] = g[owner_rows(c * 2 + 1 - core), :].astype(BF16)
            go(swap(s, c))

    def scatter_copy(s, c, slot, where):
        return remote(
            send2.at[s, c], recv2.at[s, slot], s2_send.at[s, c], s2_recv.at[s, slot], (where, mp)
        )

    def scatter_start(s):
        for c in others:
            swap(s, c).wait_recv()
            total = g[owner_rows(c * 2 + core), :] + recv1[s, c].astype(F32)
            send2[s, c] = total.astype(BF16)
            go(scatter_copy(s, c, chip, c * 2 + core))
        swap(s, chip).wait_recv()
        g[owner_rows(dp), :] += recv1[s, chip].astype(F32)

    def scatter_finish(s):
        total = g[owner_rows(dp), :]
        for c in reversed(others):
            scatter_copy(s, c, c, c * 2 + core).wait_recv()
            total = total + recv2[s, c].astype(F32)
        return total

    def adam(total):
        projected = total / total_tokens
        first = 0.9 * mom1[...] + 0.1 * projected
        second = 0.95 * mom2[...] + 0.05 * projected * projected
        mom1[...] = first
        mom2[...] = second
        return (-0.02) * (first / (jnp.sqrt(second) + 1e-08))

    def gather_copy(s, owner, sem_at, where):
        part = d_out.at[owner_rows(owner), :] if s else rall.at[block_at(owner, toks), :]
        return remote(part, part, d_send.at[s, sem_at], d_recv.at[s, owner], where)

    def gather_start(s):
        for c in others:
            go(gather_copy(s, dp, c, (c * 2 + core, mp)))
        go(gather_copy(s, dp, n_ch + chip, (partner, mp)))

    def gather_forward(s):
        for c in reversed(others):
            owner = c * 2 + core
            gather_copy(s, owner, c, (owner, mp)).wait_recv()
            go(gather_copy(s, owner, n_ch + c, (partner, mp)))

    def gathered(s, c):
        gather_copy(s, c * 2 + 1 - core, n_ch + c, (partner, mp)).wait_recv()

    def lift(c, at):
        both = block_at(c, 2 * rows)
        put = block_at(at, 2 * rows)
        for j in range(n_mp):
            cols = slice(j * fin, (j + 1) * fin)
            lifted = dot_nt(d_out[both, :], b[cols, :])
            w_out[put, cols] = (w[j, both, :].astype(F32) + lifted).astype(BF16)

    x1_copy.wait()
    b_copies[0].wait()
    rpart[...] = jnp.dot(x1[...], b[columns(mp), :], preferred_element_type=F32)
    for q in range(n_mp):
        zsend[q] = rpart[q * piece:(q + 1) * piece, :].astype(BF16)
    if window > chunk:
        cpad[...] = jnp.zeros_like(cpad)
    x0_copy.wait()
    pl.semaphore_wait(barrier, len(peers))

    def reduce_copy(q, slot, where):
        return remote(
            zsend.at[q], zrecv.at[slot], z_send.at[0, q], z_recv.at[0, slot], (dp, where)
        )

    def mine(q):
        at = dp * toks + q * piece
        return rall.at[pl.ds(pl.multiple_of(at, piece), piece), :]

    def spread_copy(q, lane, where):
        return remote(mine(q), mine(q), z_send.at[1, lane], z_recv.at[1, q], (dp, where))

    for k in range(1, n_mp):
        go(reduce_copy(mp_at(k), mp, mp_at(k)))
    xs.own(True)
    for copy in b_copies[1:]:
        copy.wait()
    for copy in w_copies:
        copy.wait()
    block(mp, True)
    total = rpart[block_at(mp, piece), :]
    for k in range(1, n_mp):
        q = mp_at(k)
        reduce_copy(q, q, q).wait_recv()
        total = total + zrecv[q].astype(F32)
    mine(mp)[...] = total.astype(BF16)
    for k in range(1, n_mp):
        go(spread_copy(mp, k, mp_at(k)))

    paired = len(order[:2]) * xs.parts
    pl.when(inner)(lambda: xs.forward(xs.hops[:paired]))
    for k in range(1, n_mp):
        q = mp_at(k)
        spread_copy(q, k, q).wait_recv()

    def reduced1():
        return rall[block_at(dp, toks), :]

    for i in range(tiles):
        at = slice(i * tile, (i + 1) * tile)
        g[at, :] = dot_tn(x1[:, at], reduced1())
        swap_start(2, i)
    pl.when(inner)(lambda: xs.forward(xs.hops[paired:paired + 1]))
    scatter_start(2)
    gather_start(0)
    pl.when(inner)(lambda: xs.forward(xs.hops[paired + 1:]))
    for i in order[:-1]:
        pl.when(outer)(lambda i=i: xs.pull(i))
        block(other_at(i), False)
    total = scatter_finish(2)
    cpad[mp, pl.ds(pl.multiple_of(inside, chunk), chunk), :] = total.astype(BF16)
    cs.own(True)
    gather_forward(0)
    pl.when(outer)(lambda: xs.pull(order[-1]))
    block(other_at(order[-1]), False)
    t_copy.wait()
    reduced = r[...].astype(BF16)
    for i in range(tiles):
        at = slice(i * tile, (i + 1) * tile)
        outputs = y[:, at].astype(BF16).astype(F32)
        e = (outputs - tgt[0, :, at].astype(F32)).astype(BF16)
        g[at, :] = dot_tn(e, reduced)
        swap_start(0, i)
    m_copy.wait()
    v_copy.wait()
    paired = len(order[:2]) * cs.parts
    pl.when(inner)(lambda: cs.forward(cs.hops[:paired]))
    scatter_start(0)
    pl.when(inner)(lambda: cs.forward(cs.hops[paired:]))
    for c in range(n_ch):
        gathered(0, c)
    gram = dot_tn(rall[...], rall[...]).astype(BF16)
    d0[...] = adam(scatter_finish(0)).astype(BF16)
    corr[...] = jnp.dot(d0[...], gram, preferred_element_type=F32)

    def span(j, at):
        return jnp.dot(
            w[j, at, pl.ds(pl.multiple_of(start, window), window)], cpad[j],
            preferred_element_type=F32,
        )

    for i in order[:-1]:
        pl.when(outer)(lambda i=i: cs.pull(i))
    for i in range(tiles):
        at = slice(i * tile, (i + 1) * tile)
        total = span(mp, at) - dot_tn(tgt[1, :, at], reduced1())
        for k in order[:-1]:
            total = total + span(other_at(k), at)
        g[at, :] = total
    pl.when(outer)(lambda: cs.pull(order[-1]))
    for i in range(tiles):
        at = slice(i * tile, (i + 1) * tile)
        g[at, :] += span(other_at(order[-1]), at)
        swap_start(1, i)
    scatter_start(1)
    step = adam(scatter_finish(1) + corr[...])
    d_out[owner_rows(dp), :] = (d0[...].astype(F32) + step).astype(BF16)
    gather_start(1)
    m_done = pltpu.make_async_copy(mom1, m_out.at[0], o_sem.at[0])
    v_done = pltpu.make_async_copy(mom2, v_out.at[0], o_sem.at[1])
    m_done.start()
    v_done.start()
    gathered(1, chip)
    lift(chip, side)
    gather_forward(1)
    gathered(1, near)
    lift(near, 1 - side)
    for c in others[:-1]:
        gathered(1, c)
    for copy in sends:
        copy.wait_send()
    xs.sent()
    cs.sent()
    m_done.wait()
    v_done.wait()


def last_lift(n_dp, width, w, mine, d, b, first, second, w_out, m_out, v_out, stage, sem, s_sem):
    out_rows, features = w.shape
    deep = mine.shape[0]
    n_pairs = out_rows // deep
    pair = lax.div(lax.axis_index("dp"), 4)

    def rows_of(q):
        return pl.ds(pl.multiple_of(q * deep, deep), deep)

    copies = [
        pltpu.make_async_copy(mine, w_out.at[rows_of(pair)], s_sem.at[0]),
        pltpu.make_async_copy(first, m_out, s_sem.at[1]),
        pltpu.make_async_copy(second, v_out, s_sem.at[2]),
    ]
    for copy in copies:
        copy.start()
    for k in range(1, n_pairs):
        rows = rows_of(lax.rem(pair + k, n_pairs))
        for i in range(features // width):
            at = slice(i * width, (i + 1) * width)
            lifted = dot_nt(d[rows, :], b[at, :])
            stage[k - 1, :, at] = (w[rows, at].astype(F32) + lifted).astype(BF16)
            copy = pltpu.make_async_copy(
                stage.at[k - 1, :, at], w_out.at[rows, at], sem.at[k - 1, i]
            )
            copy.start()
            copies.append(copy)
    for copy in copies:
        copy.wait()


def local(n_dp, n_mp, tokens, targets, weight, basis, moment1, moment2):
    steps, toks, fin = tokens.shape
    out_rows, features = weight.shape
    rank = basis.shape[1]
    rows = moment1.shape[1]
    n_ch = n_dp // 2
    hbm = pl.BlockSpec(memory_space=pltpu.HBM)
    vmem = pl.BlockSpec(memory_space=pltpu.VMEM)
    anywhere = pl.BlockSpec(memory_space=pl.ANY)
    dma = pltpu.SemaphoreType.DMA
    mine, d, first, second = pl.pallas_call(
        functools.partial(kernel, n_dp, n_mp, toks * n_dp),
        out_shape=(
            jax.ShapeDtypeStruct((4 * rows, features), BF16),
            jax.ShapeDtypeStruct((out_rows, rank), BF16),
            jax.ShapeDtypeStruct((1, rows, rank), F32),
            jax.ShapeDtypeStruct((1, rows, rank), F32),
        ),
        in_specs=[hbm] * 6,
        out_specs=(vmem, vmem, anywhere, anywhere),
        scratch_shapes=[
            pltpu.VMEM((n_mp, toks, fin), BF16),
            pltpu.VMEM((toks, fin), BF16),
            pltpu.VMEM((steps, toks, out_rows), BF16),
            pltpu.VMEM((n_mp, out_rows, fin), BF16),
            pltpu.VMEM((features, rank), BF16),
            pltpu.VMEM((rows, rank), F32),
            pltpu.VMEM((rows, rank), F32),
            pltpu.VMEM((toks, out_rows), F32),
            pltpu.VMEM((toks, rank), F32),
            pltpu.VMEM((out_rows, rank), F32),
            pltpu.VMEM((3, n_ch, rows, rank), BF16),
            pltpu.VMEM((3, n_ch, rows, rank), BF16),
            pltpu.VMEM((3, n_ch, rows, rank), BF16),
            pltpu.VMEM((3, n_ch, rows, rank), BF16),
            pltpu.VMEM((n_dp * toks, rank), BF16),
            pltpu.VMEM((toks, rank), F32),
            pltpu.VMEM((n_mp, toks // n_mp, rank), BF16),
            pltpu.VMEM((n_mp, toks // n_mp, rank), BF16),
            pltpu.VMEM((n_mp, max(128, fin // n_dp), rank), BF16),
            pltpu.VMEM((rows, rank), BF16),
            pltpu.VMEM((rows, rank), F32),
            dma((2 * n_mp + 5,)),
            dma((n_mp + 1, 2)),
            dma((n_mp, 2)),
            dma((n_mp + 1, 2)),
            dma((n_mp, 2)),
            dma((2, n_mp)),
            dma((2, n_mp)),
            dma((3, n_ch)),
            dma((3, n_ch)),
            dma((3, n_ch)),
            dma((3, n_ch)),
            dma((2, n_dp)),
            dma((2, n_dp)),
            dma((2,)),
        ],
        compiler_params=pltpu.CompilerParams(
            collective_id=0, has_side_effects=True, vmem_limit_bytes=36 * 2**20
        ),
    )(*[
        pltpu.with_memory_space_constraint(x, pltpu.HBM)
        for x in (tokens, targets, weight, basis, moment1, moment2)
    ])
    width = min(512, features)
    return pl.pallas_call(
        functools.partial(last_lift, n_dp, width),
        out_shape=(
            jax.ShapeDtypeStruct((out_rows, features), BF16),
            jax.ShapeDtypeStruct((1, rows, rank), F32),
            jax.ShapeDtypeStruct((1, rows, rank), F32),
        ),
        in_specs=[vmem] * 6,
        out_specs=(hbm,) * 3,
        scratch_shapes=[
            pltpu.VMEM((n_ch // 2 - 1, 4 * rows, features), BF16),
            dma((n_ch // 2 - 1, features // width)),
            dma((3,)),
        ],
        compiler_params=pltpu.CompilerParams(vmem_limit_bytes=12 * 2**20),
    )(weight, mine, d, basis, first, second)


def solution(mesh):
    in_specs = (
        P(None, "dp", "mp"),
        P(None, "dp", "mp"),
        P("mp", None),
        P(),
        P("mp", "dp", None),
        P("mp", "dp", None),
    )
    out_specs = (P("mp", None), P("mp", "dp", None), P("mp", "dp", None))
    body = functools.partial(local, mesh.shape["dp"], mesh.shape["mp"])
    return jax.shard_map(body, mesh=mesh, in_specs=in_specs, out_specs=out_specs, check_vma=False)
```

```python
import functools

import jax
import jax.numpy as jnp
from jax import lax
from jax.experimental import pallas as pl
from jax.experimental.pallas import tpu as pltpu
from jax.sharding import PartitionSpec as P

F32 = jnp.float32
BF16 = jnp.bfloat16


def dot_nt(a, b):
    return lax.dot_general(a, b, (((1,), (1,)), ((), ())), preferred_element_type=F32)


def dot_tn(a, b):
    return lax.dot_general(a, b, (((0,), (0,)), ((), ())), preferred_element_type=F32)


def kernel(
    n_dp, n_mp, total_tokens,
    tok, tgt_hbm, w_hbm, b_hbm, m_hbm, v_hbm,
    w_out, d_out, m_out, v_out,
    xbuf, x1, tgt, w, b, mom1, mom2, y, r, g, send1, recv1, send2, recv2,
    rall, rpart, zsend, zrecv, cpad, d0, corr,
    l_sem, x_send, x_recv, c_send, c_recv, z_send, z_recv,
    s1_send, s1_recv, s2_send, s2_recv, d_send, d_recv, o_sem,
):
    dp = lax.axis_index("dp")
    mp = lax.axis_index("mp")
    core = lax.rem(dp, 2)
    chip = lax.div(dp, 2)
    side = lax.rem(chip, 2)
    pair = lax.div(chip, 2)
    partner = dp + 1 - 2 * core
    n_ch = n_dp // 2
    n_pairs = n_ch // 2
    toks = x1.shape[0]
    out_rows, features = w_hbm.shape
    rows = out_rows // n_dp
    fin = features // n_mp
    piece = toks // n_mp
    chunk = fin // n_dp
    window = cpad.shape[1]
    start = lax.div(dp * chunk, window) * window
    inside = dp * chunk - start
    tile = min(512, out_rows)
    tiles = out_rows // tile
    per_tile = tile // (2 * rows)
    inner = jnp.logical_and(mp > 0, mp < n_mp - 1)
    outer = jnp.logical_not(inner)

    def mp_at(k):
        return lax.rem(mp + k, n_mp)

    near = pair * 2 + 1 - side
    others = []
    for k in range(1, n_pairs):
        q = lax.rem(pair + k, n_pairs)
        others += [q * 2 + 1 - side, q * 2 + side]
    others.append(near)

    def block_at(i, size):
        return pl.ds(pl.multiple_of(i * size, size), size)

    def columns(j):
        return block_at(j, fin)

    def owner_rows(i):
        return block_at(i, rows)

    def remote(src, dst, send, recv, where):
        return pltpu.make_async_remote_copy(
            src_ref=src, dst_ref=dst, send_sem=send, recv_sem=recv,
            device_id=where, device_id_type=pl.DeviceIdType.MESH,
        )

    loads = iter(range(l_sem.shape[0]))

    def load(src, dst):
        copy = pltpu.make_async_copy(src, dst, l_sem.at[next(loads)])
        copy.start()
        return copy

    x1_copy = load(tok.at[1], x1)
    b_copies = [load(b_hbm.at[columns(mp)], b.at[columns(mp)])]
    x0_copy = load(tok.at[0], xbuf.at[mp])

    barrier = pltpu.get_barrier_semaphore()
    peers = [(dp, mp_at(k)) for k in range(1, n_mp)]
    peers += [(c * 2 + core, mp) for c in others]
    peers += [(partner, mp)]
    for peer in peers:
        pl.semaphore_signal(barrier, inc=1, device_id=peer, device_id_type=pl.DeviceIdType.MESH)

    for k in range(1, n_mp):
        b_copies.append(load(b_hbm.at[columns(mp_at(k))], b.at[columns(mp_at(k))]))
    w_copies = [load(w_hbm.at[:, columns(mp_at(k))], w.at[mp_at(k)]) for k in range(n_mp)]
    t_copy = load(tgt_hbm, tgt)
    m_copy = load(m_hbm.at[0], mom1)
    v_copy = load(v_hbm.at[0], mom2)
    sends = []

    def go(copy):
        copy.start()
        sends.append(copy)

    low = (mp < n_mp // 2).astype(jnp.int32)

    def other_at(i):
        down = n_mp - 1 - i
        down = down - (down <= mp).astype(jnp.int32)
        up = i + (mp <= i).astype(jnp.int32)
        return low * down + (1 - low) * up

    order = list(reversed(range(n_mp - 1)))

    class Relay:
        def __init__(self, at, parts, send, recv):
            self.at, self.parts, self.send, self.recv = at, parts, send, recv
            self.hops = [(i, c) for c in range(parts) for i in order[:2]]
            self.hops += [(i, c) for i in order[2:] for c in range(parts)]

        def copy(self, j, lane, c, where):
            part = self.at(j, c)
            return remote(part, part, self.send.at[lane, c], self.recv.at[j, c], (dp, where))

        def own(self, act):
            for c in range(self.parts):
                for lane, (onward, to) in enumerate(((mp > 0, mp - 1), (mp < n_mp - 1, mp + 1))):
                    copy = self.copy(mp, lane, c, to)
                    pl.when(onward)(copy.start if act else copy.wait_send)

        def hop(self, i, c):
            j = other_at(i)
            below = (j > mp).astype(jnp.int32)
            to = mp + 1 - 2 * below
            onward = jnp.logical_and(to >= 0, to < n_mp)
            return onward, self.copy(j, 2 + i, c, to)

        def forward(self, hops):
            for i, c in hops:
                onward, copy = self.hop(i, c)
                copy.wait_recv()
                pl.when(onward)(copy.start)

        def pull(self, i):
            self.forward([(i, c) for c in range(self.parts)])

        def sent(self):
            self.own(False)
            for i, c in self.hops:
                onward, copy = self.hop(i, c)
                pl.when(onward)(copy.wait_send)

    half = toks // 2
    xs = Relay(lambda j, c: xbuf.at[j, c * half:(c + 1) * half], 2, x_send, x_recv)
    def c_copy(j, lane, where):
        part = cpad.at[j, pl.ds(pl.multiple_of(inside, chunk), chunk)]
        return remote(part, part, c_send.at[lane], c_recv.at[j], (dp, where))

    def block(j, first):
        x = xbuf[j]
        for i in range(tiles):
            at = slice(i * tile, (i + 1) * tile)
            term = dot_nt(x, w[j, at, :])
            if first:
                y[:, at] = term
            else:
                y[:, at] += term
        term = jnp.dot(x, b[columns(j), :], preferred_element_type=F32)
        if first:
            r[...] = term
        else:
            r[...] += term

    def swap(s, c):
        return remote(
            send1.at[s, c], recv1.at[s, c], s1_send.at[s, c], s1_recv.at[s, c], (partner, mp)
        )

    def swap_start(s, chips):
        for c in chips:
            send1[s, c] = g[min(s, 1), owner_rows(c * 2 + 1 - core), :].astype(BF16)
            go(swap(s, c))

    def tile_chips(i):
        return range(i * per_tile, (i + 1) * per_tile)

    def scatter_copy(s, c, slot, where):
        return remote(
            send2.at[s, c], recv2.at[s, slot], s2_send.at[s, c], s2_recv.at[s, slot], (where, mp)
        )

    def scatter_start(s):
        for c in others:
            swap(s, c).wait_recv()
            total = g[min(s, 1), owner_rows(c * 2 + core), :] + recv1[s, c].astype(F32)
            send2[s, c] = total.astype(BF16)
            go(scatter_copy(s, c, chip, c * 2 + core))
        swap(s, chip).wait_recv()
        g[min(s, 1), owner_rows(dp), :] += recv1[s, chip].astype(F32)

    def scatter_finish(s):
        total = g[min(s, 1), owner_rows(dp), :]
        for c in reversed(others):
            scatter_copy(s, c, c, c * 2 + core).wait_recv()
            total = total + recv2[s, c].astype(F32)
        return total

    def adam(total):
        projected = total / total_tokens
        first = 0.9 * mom1[...] + 0.1 * projected
        second = 0.95 * mom2[...] + 0.05 * projected * projected
        mom1[...] = first
        mom2[...] = second
        return (-0.02) * (first / (jnp.sqrt(second) + 1e-08))

    def gather_copy(s, owner, sem_at, where):
        part = d_out.at[owner_rows(owner), :] if s else rall.at[block_at(owner, toks), :]
        return remote(part, part, d_send.at[s, sem_at], d_recv.at[s, owner], where)

    def gather_start(s):
        for c in others:
            go(gather_copy(s, dp, c, (c * 2 + core, mp)))
        go(gather_copy(s, dp, n_ch + chip, (partner, mp)))

    def gather_forward(s, chips):
        for c in chips:
            owner = c * 2 + core
            gather_copy(s, owner, c, (owner, mp)).wait_recv()
            go(gather_copy(s, owner, n_ch + c, (partner, mp)))

    def gathered(s, c):
        gather_copy(s, c * 2 + 1 - core, n_ch + c, (partner, mp)).wait_recv()

    def lift(first, at, count):
        both = pl.ds(pl.multiple_of(first * rows, rows), count * rows)
        put = pl.ds(pl.multiple_of(at * rows, rows), count * rows)
        for j in range(n_mp):
            cols = slice(j * fin, (j + 1) * fin)
            lifted = dot_nt(d_out[both, :], b[cols, :])
            w_out[put, cols] = (w[j, both, :].astype(F32) + lifted).astype(BF16)

    x1_copy.wait()
    b_copies[0].wait()
    rpart[...] = jnp.dot(x1[...], b[columns(mp), :], preferred_element_type=F32)
    for q in range(n_mp):
        zsend[q] = rpart[q * piece:(q + 1) * piece, :].astype(BF16)
    if window > chunk:
        cpad[...] = jnp.zeros_like(cpad)
    x0_copy.wait()
    pl.semaphore_wait(barrier, len(peers))

    def reduce_copy(q, slot, where):
        return remote(
            zsend.at[q], zrecv.at[slot], z_send.at[0, q], z_recv.at[0, slot], (dp, where)
        )

    def mine(q):
        at = dp * toks + q * piece
        return rall.at[pl.ds(pl.multiple_of(at, piece), piece), :]

    def spread_copy(q, lane, where):
        return remote(mine(q), mine(q), z_send.at[1, lane], z_recv.at[1, q], (dp, where))

    for k in range(1, n_mp):
        go(reduce_copy(mp_at(k), mp, mp_at(k)))
    xs.own(True)
    total = rpart[block_at(mp, piece), :]
    for k in range(1, n_mp):
        q = mp_at(k)
        reduce_copy(q, q, q).wait_recv()
        total = total + zrecv[q].astype(F32)
    mine(mp)[...] = total.astype(BF16)
    for k in range(1, n_mp):
        go(spread_copy(mp, k, mp_at(k)))

    n_first = len(order[:2])
    cuts = [0, n_first, n_first * xs.parts, len(xs.hops)]

    def relay(i):
        pl.when(inner)(lambda: xs.forward(xs.hops[cuts[i]:cuts[i + 1]]))

    relay(0)
    for k in range(1, n_mp):
        q = mp_at(k)
        spread_copy(q, k, q).wait_recv()

    def reduced1():
        return rall[block_at(dp, toks), :]

    for i in range(tiles):
        at = slice(i * tile, (i + 1) * tile)
        g[1, at, :] = dot_tn(x1[:, at], reduced1())
        swap_start(2, tile_chips(i))
    relay(1)
    scatter_start(2)
    relay(2)
    for copy in b_copies[1:]:
        copy.wait()
    for copy in w_copies:
        copy.wait()
    block(mp, True)
    for i in order[:-1]:
        pl.when(outer)(lambda i=i: xs.pull(i))
        block(other_at(i), False)
    total = scatter_finish(2)
    cpad[mp, pl.ds(pl.multiple_of(inside, chunk), chunk), :] = total.astype(BF16)
    for i in reversed(order):
        go(c_copy(mp, i, other_at(i)))
    gather_start(0)
    pl.when(outer)(lambda: xs.pull(order[-1]))
    block(other_at(order[-1]), False)
    t_copy.wait()
    reduced = r[...].astype(BF16)
    for i in range(tiles):
        at = slice(i * tile, (i + 1) * tile)
        outputs = y[:, at].astype(BF16).astype(F32)
        e = (outputs - tgt[0, :, at].astype(F32)).astype(BF16)
        g[0, at, :] = dot_tn(e, reduced)
        swap_start(0, tile_chips(i))

    def span(j, at):
        return jnp.dot(
            w[j, at, pl.ds(pl.multiple_of(start, window), window)], cpad[j],
            preferred_element_type=F32,
        )

    for i in range(tiles):
        at = slice(i * tile, (i + 1) * tile)
        g[1, at, :] = span(mp, at) - dot_tn(tgt[1, :, at], reduced1())
    gather_forward(0, reversed(others))
    scatter_start(0)
    for k in order[:-1]:
        c_copy(other_at(k), k, mp).wait_recv()
        for i in range(tiles):
            at = slice(i * tile, (i + 1) * tile)
            g[1, at, :] += span(other_at(k), at)
    c_copy(other_at(order[-1]), order[-1], mp).wait_recv()
    for c in others + [chip]:
        at = block_at(c, 2 * rows)
        g[1, at, :] += span(other_at(order[-1]), at)
        swap_start(1, [c])
    scatter_start(1)
    for c in range(n_ch):
        gathered(0, c)
    gram = dot_tn(rall[...], rall[...]).astype(BF16)
    m_copy.wait()
    v_copy.wait()
    d0[...] = adam(scatter_finish(0)).astype(BF16)
    corr[...] = jnp.dot(d0[...], gram, preferred_element_type=F32)
    step = adam(scatter_finish(1) + corr[...])
    d_out[owner_rows(dp), :] = (d0[...].astype(F32) + step).astype(BF16)
    gather_start(1)
    m_done = pltpu.make_async_copy(mom1, m_out.at[0], o_sem.at[0])
    v_done = pltpu.make_async_copy(mom2, v_out.at[0], o_sem.at[1])
    m_done.start()
    v_done.start()
    gathered(1, chip)
    lift(chip * 2, side * 2, 2)
    arrivals = list(reversed(others))
    gather_forward(1, arrivals[:-1])
    lift(near * 2 + core, (1 - side) * 2 + core, 1)
    gathered(1, near)
    lift(near * 2 + 1 - core, (1 - side) * 2 + 1 - core, 1)
    gather_forward(1, arrivals[-1:])
    for c in others[:-1]:
        gathered(1, c)
    for copy in sends:
        copy.wait_send()
    xs.sent()
    m_done.wait()
    v_done.wait()


def last_lift(n_dp, width, w, mine, d, b, first, second, w_out, m_out, v_out, stage, sem, s_sem):
    out_rows, features = w.shape
    deep = mine.shape[0]
    n_pairs = out_rows // deep
    pair = lax.div(lax.axis_index("dp"), 4)

    def rows_of(q):
        return pl.ds(pl.multiple_of(q * deep, deep), deep)

    copies = [
        pltpu.make_async_copy(mine, w_out.at[rows_of(pair)], s_sem.at[0]),
        pltpu.make_async_copy(first, m_out, s_sem.at[1]),
        pltpu.make_async_copy(second, v_out, s_sem.at[2]),
    ]
    for copy in copies:
        copy.start()
    for k in range(1, n_pairs):
        rows = rows_of(lax.rem(pair + k, n_pairs))
        for i in range(features // width):
            at = slice(i * width, (i + 1) * width)
            lifted = dot_nt(d[rows, :], b[at, :])
            stage[k - 1, :, at] = (w[rows, at].astype(F32) + lifted).astype(BF16)
            copy = pltpu.make_async_copy(
                stage.at[k - 1, :, at], w_out.at[rows, at], sem.at[k - 1, i]
            )
            copy.start()
            copies.append(copy)
    for copy in copies:
        copy.wait()


def local(n_dp, n_mp, tokens, targets, weight, basis, moment1, moment2):
    steps, toks, fin = tokens.shape
    out_rows, features = weight.shape
    rank = basis.shape[1]
    rows = moment1.shape[1]
    n_ch = n_dp // 2
    hbm = pl.BlockSpec(memory_space=pltpu.HBM)
    vmem = pl.BlockSpec(memory_space=pltpu.VMEM)
    anywhere = pl.BlockSpec(memory_space=pl.ANY)
    dma = pltpu.SemaphoreType.DMA
    mine, d, first, second = pl.pallas_call(
        functools.partial(kernel, n_dp, n_mp, toks * n_dp),
        out_shape=(
            jax.ShapeDtypeStruct((4 * rows, features), BF16),
            jax.ShapeDtypeStruct((out_rows, rank), BF16),
            jax.ShapeDtypeStruct((1, rows, rank), F32),
            jax.ShapeDtypeStruct((1, rows, rank), F32),
        ),
        in_specs=[hbm] * 6,
        out_specs=(vmem, vmem, anywhere, anywhere),
        scratch_shapes=[
            pltpu.VMEM((n_mp, toks, fin), BF16),
            pltpu.VMEM((toks, fin), BF16),
            pltpu.VMEM((steps, toks, out_rows), BF16),
            pltpu.VMEM((n_mp, out_rows, fin), BF16),
            pltpu.VMEM((features, rank), BF16),
            pltpu.VMEM((rows, rank), F32),
            pltpu.VMEM((rows, rank), F32),
            pltpu.VMEM((toks, out_rows), F32),
            pltpu.VMEM((toks, rank), F32),
            pltpu.VMEM((2, out_rows, rank), F32),
            pltpu.VMEM((3, n_ch, rows, rank), BF16),
            pltpu.VMEM((3, n_ch, rows, rank), BF16),
            pltpu.VMEM((3, n_ch, rows, rank), BF16),
            pltpu.VMEM((3, n_ch, rows, rank), BF16),
            pltpu.VMEM((n_dp * toks, rank), BF16),
            pltpu.VMEM((toks, rank), F32),
            pltpu.VMEM((n_mp, toks // n_mp, rank), BF16),
            pltpu.VMEM((n_mp, toks // n_mp, rank), BF16),
            pltpu.VMEM((n_mp, max(128, fin // n_dp), rank), BF16),
            pltpu.VMEM((rows, rank), BF16),
            pltpu.VMEM((rows, rank), F32),
            dma((2 * n_mp + 5,)),
            dma((n_mp + 1, 2)),
            dma((n_mp, 2)),
            dma((n_mp,)),
            dma((n_mp,)),
            dma((2, n_mp)),
            dma((2, n_mp)),
            dma((3, n_ch)),
            dma((3, n_ch)),
            dma((3, n_ch)),
            dma((3, n_ch)),
            dma((2, n_dp)),
            dma((2, n_dp)),
            dma((2,)),
        ],
        compiler_params=pltpu.CompilerParams(
            collective_id=0, has_side_effects=True, vmem_limit_bytes=38 * 2**20
        ),
    )(*[
        pltpu.with_memory_space_constraint(x, pltpu.HBM)
        for x in (tokens, targets, weight, basis, moment1, moment2)
    ])
    width = min(512, features)
    return pl.pallas_call(
        functools.partial(last_lift, n_dp, width),
        out_shape=(
            jax.ShapeDtypeStruct((out_rows, features), BF16),
            jax.ShapeDtypeStruct((1, rows, rank), F32),
            jax.ShapeDtypeStruct((1, rows, rank), F32),
        ),
        in_specs=[vmem] * 6,
        out_specs=(hbm,) * 3,
        scratch_shapes=[
            pltpu.VMEM((n_ch // 2 - 1, 4 * rows, features), BF16),
            dma((n_ch // 2 - 1, features // width)),
            dma((3,)),
        ],
        compiler_params=pltpu.CompilerParams(vmem_limit_bytes=12 * 2**20),
    )(weight, mine, d, basis, first, second)


def solution(mesh):
    in_specs = (
        P(None, "dp", "mp"),
        P(None, "dp", "mp"),
        P("mp", None),
        P(),
        P("mp", "dp", None),
        P("mp", "dp", None),
    )
    out_specs = (P("mp", None), P("mp", "dp", None), P("mp", "dp", None))
    body = functools.partial(local, mesh.shape["dp"], mesh.shape["mp"])
    return jax.shard_map(body, mesh=mesh, in_specs=in_specs, out_specs=out_specs, check_vma=False)
```

```python
import functools

import jax
import jax.numpy as jnp
from jax import lax
from jax.experimental import pallas as pl
from jax.experimental.pallas import tpu as pltpu
from jax.sharding import PartitionSpec as P

F32 = jnp.float32
BF16 = jnp.bfloat16


def dot_nt(a, b):
    return lax.dot_general(a, b, (((1,), (1,)), ((), ())), preferred_element_type=F32)


def dot_tn(a, b):
    return lax.dot_general(a, b, (((0,), (0,)), ((), ())), preferred_element_type=F32)


def kernel(
    n_dp, n_mp, total_tokens,
    tok, tgt_hbm, w_hbm, b_hbm, m_hbm, v_hbm,
    w_out, d_out, m_out, v_out,
    xbuf, x1, tgt, w, b, mom1, mom2, y, r, g, send1, recv1, send2, recv2,
    rall, rpart, zsend, zrecv, cpad, d0, corr,
    l_sem, x_send, x_recv, c_send, c_recv, z_send, z_recv,
    s1_send, s1_recv, s2_send, s2_recv, d_send, d_recv, o_sem,
):
    dp = lax.axis_index("dp")
    mp = lax.axis_index("mp")
    core = lax.rem(dp, 2)
    chip = lax.div(dp, 2)
    side = lax.rem(chip, 2)
    pair = lax.div(chip, 2)
    partner = dp + 1 - 2 * core
    n_ch = n_dp // 2
    n_pairs = n_ch // 2
    toks = x1.shape[0]
    out_rows, features = w_hbm.shape
    rows = out_rows // n_dp
    fin = features // n_mp
    piece = toks // n_mp
    chunk = fin // n_dp
    window = cpad.shape[1]
    start = lax.div(dp * chunk, window) * window
    inside = dp * chunk - start
    tile = min(512, out_rows)
    tiles = out_rows // tile
    per_tile = tile // (2 * rows)
    inner = jnp.logical_and(mp > 0, mp < n_mp - 1)
    outer = jnp.logical_not(inner)

    def mp_at(k):
        return lax.rem(mp + k, n_mp)

    near = pair * 2 + 1 - side
    others = []
    for k in range(1, n_pairs):
        q = lax.rem(pair + k, n_pairs)
        others += [q * 2 + 1 - side, q * 2 + side]
    others.append(near)

    def block_at(i, size):
        return pl.ds(pl.multiple_of(i * size, size), size)

    def columns(j):
        return block_at(j, fin)

    def owner_rows(i):
        return block_at(i, rows)

    def remote(src, dst, send, recv, where):
        return pltpu.make_async_remote_copy(
            src_ref=src, dst_ref=dst, send_sem=send, recv_sem=recv,
            device_id=where, device_id_type=pl.DeviceIdType.MESH,
        )

    loads = iter(range(l_sem.shape[0]))

    def load(src, dst):
        copy = pltpu.make_async_copy(src, dst, l_sem.at[next(loads)])
        copy.start()
        return copy

    x1_copy = load(tok.at[1], x1)
    b_copies = [load(b_hbm.at[columns(mp)], b.at[columns(mp)])]
    x0_copy = load(tok.at[0], xbuf.at[mp])

    barrier = pltpu.get_barrier_semaphore()
    peers = [(dp, mp_at(k)) for k in range(1, n_mp)]
    peers += [(c * 2 + core, mp) for c in others]
    peers += [(partner, mp)]
    for peer in peers:
        pl.semaphore_signal(barrier, inc=1, device_id=peer, device_id_type=pl.DeviceIdType.MESH)

    for k in range(1, n_mp):
        b_copies.append(load(b_hbm.at[columns(mp_at(k))], b.at[columns(mp_at(k))]))
    w_copies = [load(w_hbm.at[:, columns(mp_at(k))], w.at[mp_at(k)]) for k in range(n_mp)]
    t_copy = load(tgt_hbm, tgt)
    m_copy = load(m_hbm.at[0], mom1)
    v_copy = load(v_hbm.at[0], mom2)
    sends = []

    def go(copy):
        copy.start()
        sends.append(copy)

    low = (mp < n_mp // 2).astype(jnp.int32)

    def other_at(i):
        down = n_mp - 1 - i
        down = down - (down <= mp).astype(jnp.int32)
        up = i + (mp <= i).astype(jnp.int32)
        return low * down + (1 - low) * up

    order = list(reversed(range(n_mp - 1)))

    class Relay:
        def __init__(self, at, parts, send, recv):
            self.at, self.parts, self.send, self.recv = at, parts, send, recv
            self.hops = [(i, c) for c in range(parts) for i in order[:2]]
            self.hops += [(i, c) for i in order[2:] for c in range(parts)]

        def copy(self, j, lane, c, where):
            part = self.at(j, c)
            return remote(part, part, self.send.at[lane, c], self.recv.at[j, c], (dp, where))

        def own(self, act):
            for c in range(self.parts):
                for lane, (onward, to) in enumerate(((mp > 0, mp - 1), (mp < n_mp - 1, mp + 1))):
                    copy = self.copy(mp, lane, c, to)
                    pl.when(onward)(copy.start if act else copy.wait_send)

        def hop(self, i, c):
            j = other_at(i)
            below = (j > mp).astype(jnp.int32)
            to = mp + 1 - 2 * below
            onward = jnp.logical_and(to >= 0, to < n_mp)
            return onward, self.copy(j, 2 + i, c, to)

        def forward(self, hops):
            for i, c in hops:
                onward, copy = self.hop(i, c)
                copy.wait_recv()
                pl.when(onward)(copy.start)

        def pull(self, i):
            self.forward([(i, c) for c in range(self.parts)])

        def sent(self):
            self.own(False)
            for i, c in self.hops:
                onward, copy = self.hop(i, c)
                pl.when(onward)(copy.wait_send)

    half = toks // 2
    xs = Relay(lambda j, c: xbuf.at[j, c * half:(c + 1) * half], 2, x_send, x_recv)
    c_parts = 2 if chunk % 32 == 0 else 1
    c_size = chunk // c_parts
    cs = Relay(
        lambda j, c: cpad.at[j, pl.ds(pl.multiple_of(inside + c * c_size, c_size), c_size)],
        c_parts, c_send, c_recv,
    )

    def block(j, first):
        x = xbuf[j]
        for i in range(tiles):
            at = slice(i * tile, (i + 1) * tile)
            term = dot_nt(x, w[j, at, :])
            if first:
                y[:, at] = term
            else:
                y[:, at] += term
        term = jnp.dot(x, b[columns(j), :], preferred_element_type=F32)
        if first:
            r[...] = term
        else:
            r[...] += term

    def swap(s, c):
        return remote(
            send1.at[s, c], recv1.at[s, c], s1_send.at[s, c], s1_recv.at[s, c], (partner, mp)
        )

    def swap_start(s, chips):
        for c in chips:
            send1[s, c] = g[min(s, 1), owner_rows(c * 2 + 1 - core), :].astype(BF16)
            go(swap(s, c))

    def tile_chips(i):
        return range(i * per_tile, (i + 1) * per_tile)

    def scatter_copy(s, c, slot, where):
        return remote(
            send2.at[s, c], recv2.at[s, slot], s2_send.at[s, c], s2_recv.at[s, slot], (where, mp)
        )

    def scatter_start(s):
        for c in others:
            swap(s, c).wait_recv()
            total = g[min(s, 1), owner_rows(c * 2 + core), :] + recv1[s, c].astype(F32)
            send2[s, c] = total.astype(BF16)
            go(scatter_copy(s, c, chip, c * 2 + core))
        swap(s, chip).wait_recv()
        g[min(s, 1), owner_rows(dp), :] += recv1[s, chip].astype(F32)

    def scatter_finish(s):
        total = g[min(s, 1), owner_rows(dp), :]
        for c in reversed(others):
            scatter_copy(s, c, c, c * 2 + core).wait_recv()
            total = total + recv2[s, c].astype(F32)
        return total

    def adam(total):
        projected = total / total_tokens
        first = 0.9 * mom1[...] + 0.1 * projected
        second = 0.95 * mom2[...] + 0.05 * projected * projected
        mom1[...] = first
        mom2[...] = second
        return (-0.02) * (first / (jnp.sqrt(second) + 1e-08))

    def gather_copy(s, owner, sem_at, where):
        part = d_out.at[owner_rows(owner), :] if s else rall.at[block_at(owner, toks), :]
        return remote(part, part, d_send.at[s, sem_at], d_recv.at[s, owner], where)

    def gather_start(s):
        for c in reversed(others):
            go(gather_copy(s, dp, c, (c * 2 + core, mp)))
        go(gather_copy(s, dp, n_ch + chip, (partner, mp)))

    def gather_forward(s, chips):
        for c in chips:
            owner = c * 2 + core
            gather_copy(s, owner, c, (owner, mp)).wait_recv()
            go(gather_copy(s, owner, n_ch + c, (partner, mp)))

    def gathered(s, c):
        gather_copy(s, c * 2 + 1 - core, n_ch + c, (partner, mp)).wait_recv()

    def lift(first, at, count):
        both = pl.ds(pl.multiple_of(first * rows, rows), count * rows)
        put = pl.ds(pl.multiple_of(at * rows, rows), count * rows)
        for j in range(n_mp):
            cols = slice(j * fin, (j + 1) * fin)
            lifted = dot_nt(d_out[both, :], b[cols, :])
            w_out[put, cols] = (w[j, both, :].astype(F32) + lifted).astype(BF16)

    x1_copy.wait()
    b_copies[0].wait()
    rpart[...] = jnp.dot(x1[...], b[columns(mp), :], preferred_element_type=F32)
    for q in range(n_mp):
        zsend[q] = rpart[q * piece:(q + 1) * piece, :].astype(BF16)
    if window > chunk:
        cpad[...] = jnp.zeros_like(cpad)
    x0_copy.wait()
    pl.semaphore_wait(barrier, len(peers))

    def reduce_copy(q, slot, where):
        return remote(
            zsend.at[q], zrecv.at[slot], z_send.at[0, q], z_recv.at[0, slot], (dp, where)
        )

    def mine(q):
        at = dp * toks + q * piece
        return rall.at[pl.ds(pl.multiple_of(at, piece), piece), :]

    def spread_copy(q, lane, where):
        return remote(mine(q), mine(q), z_send.at[1, lane], z_recv.at[1, q], (dp, where))

    for k in range(1, n_mp):
        go(reduce_copy(mp_at(k), mp, mp_at(k)))
    total = rpart[block_at(mp, piece), :]
    for k in range(1, n_mp):
        q = mp_at(k)
        reduce_copy(q, q, q).wait_recv()
        total = total + zrecv[q].astype(F32)
    mine(mp)[...] = total.astype(BF16)
    for k in range(1, n_mp):
        go(spread_copy(mp, k, mp_at(k)))
    xs.own(True)

    def relay(way, first, last):
        ready = len(order[:2])
        cuts = [0, ready, ready * way.parts, len(way.hops)]
        pl.when(inner)(lambda: way.forward(way.hops[cuts[first]:cuts[last]]))

    for k in range(1, n_mp):
        q = mp_at(k)
        spread_copy(q, k, q).wait_recv()

    def reduced1():
        return rall[block_at(dp, toks), :]

    gather_start(0)
    for i in range(tiles):
        at = slice(i * tile, (i + 1) * tile)
        g[1, at, :] = dot_tn(x1[:, at], reduced1())
        swap_start(2, tile_chips(i))
    relay(xs, 0, 1)
    scatter_start(2)
    relay(xs, 1, 3)
    for copy in b_copies[1:]:
        copy.wait()
    for copy in w_copies:
        copy.wait()
    block(mp, True)
    for i in order[:-1]:
        pl.when(outer)(lambda i=i: xs.pull(i))
        block(other_at(i), False)
    total = scatter_finish(2)
    cpad[mp, pl.ds(pl.multiple_of(inside, chunk), chunk), :] = total.astype(BF16)
    cs.own(True)
    gather_forward(0, reversed(others))
    pl.when(outer)(lambda: xs.pull(order[-1]))
    block(other_at(order[-1]), False)
    t_copy.wait()
    reduced = r[...].astype(BF16)
    for i in range(tiles):
        at = slice(i * tile, (i + 1) * tile)
        outputs = y[:, at].astype(BF16).astype(F32)
        e = (outputs - tgt[0, :, at].astype(F32)).astype(BF16)
        g[0, at, :] = dot_tn(e, reduced)
        swap_start(0, tile_chips(i))

    def span(j, at):
        return jnp.dot(
            w[j, at, pl.ds(pl.multiple_of(start, window), window)], cpad[j],
            preferred_element_type=F32,
        )

    for i in range(tiles):
        at = slice(i * tile, (i + 1) * tile)
        g[1, at, :] = span(mp, at) - dot_tn(tgt[1, :, at], reduced1())
    relay(cs, 0, 2)
    scatter_start(0)
    relay(cs, 2, 3)
    for k in order[:-1]:
        pl.when(outer)(lambda k=k: cs.pull(k))
        for i in range(tiles):
            at = slice(i * tile, (i + 1) * tile)
            g[1, at, :] += span(other_at(k), at)
    pl.when(outer)(lambda: cs.pull(order[-1]))
    for c in others + [chip]:
        at = block_at(c, 2 * rows)
        g[1, at, :] += span(other_at(order[-1]), at)
        swap_start(1, [c])
    scatter_start(1)
    for c in range(n_ch):
        gathered(0, c)
    gram = dot_tn(rall[...], rall[...]).astype(BF16)
    m_copy.wait()
    v_copy.wait()
    d0[...] = adam(scatter_finish(0)).astype(BF16)
    corr[...] = jnp.dot(d0[...], gram, preferred_element_type=F32)
    step = adam(scatter_finish(1) + corr[...])
    d_out[owner_rows(dp), :] = (d0[...].astype(F32) + step).astype(BF16)
    gather_start(1)
    m_done = pltpu.make_async_copy(mom1, m_out.at[0], o_sem.at[0])
    v_done = pltpu.make_async_copy(mom2, v_out.at[0], o_sem.at[1])
    m_done.start()
    v_done.start()
    gathered(1, chip)
    lift(chip * 2, side * 2, 2)
    arrivals = list(reversed(others))
    gather_forward(1, arrivals[:-1])
    gathered(1, near)
    lift(near * 2, (1 - side) * 2, 2)
    gather_forward(1, arrivals[-1:])
    for c in others[:-1]:
        gathered(1, c)
    for copy in sends:
        copy.wait_send()
    xs.sent()
    cs.sent()
    m_done.wait()
    v_done.wait()


def last_lift(n_dp, width, w, mine, d, b, first, second, w_out, m_out, v_out, stage, sem, s_sem):
    out_rows, features = w.shape
    deep = mine.shape[0]
    n_pairs = out_rows // deep
    pair = lax.div(lax.axis_index("dp"), 4)

    def rows_of(q):
        return pl.ds(pl.multiple_of(q * deep, deep), deep)

    copies = [
        pltpu.make_async_copy(mine, w_out.at[rows_of(pair)], s_sem.at[0]),
        pltpu.make_async_copy(first, m_out, s_sem.at[1]),
        pltpu.make_async_copy(second, v_out, s_sem.at[2]),
    ]
    for copy in copies:
        copy.start()
    for k in range(1, n_pairs):
        rows = rows_of(lax.rem(pair + k, n_pairs))
        for i in range(features // width):
            at = slice(i * width, (i + 1) * width)
            lifted = dot_nt(d[rows, :], b[at, :])
            stage[k - 1, :, at] = (w[rows, at].astype(F32) + lifted).astype(BF16)
            copy = pltpu.make_async_copy(
                stage.at[k - 1, :, at], w_out.at[rows, at], sem.at[k - 1, i]
            )
            copy.start()
            copies.append(copy)
    for copy in copies:
        copy.wait()


def local(n_dp, n_mp, tokens, targets, weight, basis, moment1, moment2):
    steps, toks, fin = tokens.shape
    out_rows, features = weight.shape
    rank = basis.shape[1]
    rows = moment1.shape[1]
    n_ch = n_dp // 2
    hbm = pl.BlockSpec(memory_space=pltpu.HBM)
    vmem = pl.BlockSpec(memory_space=pltpu.VMEM)
    anywhere = pl.BlockSpec(memory_space=pl.ANY)
    dma = pltpu.SemaphoreType.DMA
    mine, d, first, second = pl.pallas_call(
        functools.partial(kernel, n_dp, n_mp, toks * n_dp),
        out_shape=(
            jax.ShapeDtypeStruct((4 * rows, features), BF16),
            jax.ShapeDtypeStruct((out_rows, rank), BF16),
            jax.ShapeDtypeStruct((1, rows, rank), F32),
            jax.ShapeDtypeStruct((1, rows, rank), F32),
        ),
        in_specs=[hbm] * 6,
        out_specs=(vmem, vmem, anywhere, anywhere),
        scratch_shapes=[
            pltpu.VMEM((n_mp, toks, fin), BF16),
            pltpu.VMEM((toks, fin), BF16),
            pltpu.VMEM((steps, toks, out_rows), BF16),
            pltpu.VMEM((n_mp, out_rows, fin), BF16),
            pltpu.VMEM((features, rank), BF16),
            pltpu.VMEM((rows, rank), F32),
            pltpu.VMEM((rows, rank), F32),
            pltpu.VMEM((toks, out_rows), F32),
            pltpu.VMEM((toks, rank), F32),
            pltpu.VMEM((2, out_rows, rank), F32),
            pltpu.VMEM((3, n_ch, rows, rank), BF16),
            pltpu.VMEM((3, n_ch, rows, rank), BF16),
            pltpu.VMEM((3, n_ch, rows, rank), BF16),
            pltpu.VMEM((3, n_ch, rows, rank), BF16),
            pltpu.VMEM((n_dp * toks, rank), BF16),
            pltpu.VMEM((toks, rank), F32),
            pltpu.VMEM((n_mp, toks // n_mp, rank), BF16),
            pltpu.VMEM((n_mp, toks // n_mp, rank), BF16),
            pltpu.VMEM((n_mp, max(128, fin // n_dp), rank), BF16),
            pltpu.VMEM((rows, rank), BF16),
            pltpu.VMEM((rows, rank), F32),
            dma((2 * n_mp + 5,)),
            dma((n_mp + 1, 2)),
            dma((n_mp, 2)),
            dma((n_mp + 1, 2)),
            dma((n_mp, 2)),
            dma((2, n_mp)),
            dma((2, n_mp)),
            dma((3, n_ch)),
            dma((3, n_ch)),
            dma((3, n_ch)),
            dma((3, n_ch)),
            dma((2, n_dp)),
            dma((2, n_dp)),
            dma((2,)),
        ],
        compiler_params=pltpu.CompilerParams(
            collective_id=0, has_side_effects=True, vmem_limit_bytes=38 * 2**20
        ),
    )(*[
        pltpu.with_memory_space_constraint(x, pltpu.HBM)
        for x in (tokens, targets, weight, basis, moment1, moment2)
    ])
    width = min(512, features)
    return pl.pallas_call(
        functools.partial(last_lift, n_dp, width),
        out_shape=(
            jax.ShapeDtypeStruct((out_rows, features), BF16),
            jax.ShapeDtypeStruct((1, rows, rank), F32),
            jax.ShapeDtypeStruct((1, rows, rank), F32),
        ),
        in_specs=[vmem] * 6,
        out_specs=(hbm,) * 3,
        scratch_shapes=[
            pltpu.VMEM((n_ch // 2 - 1, 4 * rows, features), BF16),
            dma((n_ch // 2 - 1, features // width)),
            dma((3,)),
        ],
        compiler_params=pltpu.CompilerParams(vmem_limit_bytes=12 * 2**20),
    )(weight, mine, d, basis, first, second)


def solution(mesh):
    in_specs = (
        P(None, "dp", "mp"),
        P(None, "dp", "mp"),
        P("mp", None),
        P(),
        P("mp", "dp", None),
        P("mp", "dp", None),
    )
    out_specs = (P("mp", None), P("mp", "dp", None), P("mp", "dp", None))
    body = functools.partial(local, mesh.shape["dp"], mesh.shape["mp"])
    return jax.shard_map(body, mesh=mesh, in_specs=in_specs, out_specs=out_specs, check_vma=False)
```

```python
import functools

import jax
import jax.numpy as jnp
from jax import lax
from jax.experimental import pallas as pl
from jax.experimental.pallas import tpu as pltpu
from jax.sharding import PartitionSpec as P

F32 = jnp.float32
BF16 = jnp.bfloat16


def dot_nt(a, b):
    return lax.dot_general(a, b, (((1,), (1,)), ((), ())), preferred_element_type=F32)


def dot_tn(a, b):
    return lax.dot_general(a, b, (((0,), (0,)), ((), ())), preferred_element_type=F32)


def kernel(
    n_dp, n_mp, total_tokens,
    tok, tgt_hbm, w_hbm, b_hbm, m_hbm, v_hbm,
    w_out, d_out, m_out, v_out,
    xbuf, x1, tgt, w, b, mom1, mom2, y, r, g, send1, recv1, send2, recv2,
    rall, rpart, zsend, zrecv, cpad, d0, corr,
    l_sem, x_send, x_recv, c_send, c_recv, z_send, z_recv,
    s1_send, s1_recv, s2_send, s2_recv, d_send, d_recv, o_sem,
):
    dp = lax.axis_index("dp")
    mp = lax.axis_index("mp")
    core = lax.rem(dp, 2)
    chip = lax.div(dp, 2)
    side = lax.rem(chip, 2)
    pair = lax.div(chip, 2)
    partner = dp + 1 - 2 * core
    n_ch = n_dp // 2
    n_pairs = n_ch // 2
    toks = x1.shape[0]
    out_rows, features = w_hbm.shape
    rows = out_rows // n_dp
    fin = features // n_mp
    piece = toks // n_mp
    chunk = fin // n_dp
    window = cpad.shape[1]
    start = lax.div(dp * chunk, window) * window
    inside = dp * chunk - start
    tile = min(512, out_rows)
    tiles = out_rows // tile
    per_tile = tile // (2 * rows)
    inner = jnp.logical_and(mp > 0, mp < n_mp - 1)
    outer = jnp.logical_not(inner)

    def mp_at(k):
        return lax.rem(mp + k, n_mp)

    near = pair * 2 + 1 - side
    others = []
    for k in range(1, n_pairs):
        q = lax.rem(pair + k, n_pairs)
        others += [q * 2 + 1 - side, q * 2 + side]
    others.append(near)

    def block_at(i, size):
        return pl.ds(pl.multiple_of(i * size, size), size)

    def columns(j):
        return block_at(j, fin)

    def owner_rows(i):
        return block_at(i, rows)

    def remote(src, dst, send, recv, where):
        return pltpu.make_async_remote_copy(
            src_ref=src, dst_ref=dst, send_sem=send, recv_sem=recv,
            device_id=where, device_id_type=pl.DeviceIdType.MESH,
        )

    loads = iter(range(l_sem.shape[0]))

    def load(src, dst):
        copy = pltpu.make_async_copy(src, dst, l_sem.at[next(loads)])
        copy.start()
        return copy

    x1_copy = load(tok.at[1], x1)
    b_copies = [load(b_hbm.at[columns(mp)], b.at[columns(mp)])]
    x0_copy = load(tok.at[0], xbuf.at[mp])

    barrier = pltpu.get_barrier_semaphore()
    peers = [(dp, mp_at(k)) for k in range(1, n_mp)]
    peers += [(c * 2 + core, mp) for c in others]
    peers += [(partner, mp)]
    for peer in peers:
        pl.semaphore_signal(barrier, inc=1, device_id=peer, device_id_type=pl.DeviceIdType.MESH)

    for k in range(1, n_mp):
        b_copies.append(load(b_hbm.at[columns(mp_at(k))], b.at[columns(mp_at(k))]))
    w_copies = [load(w_hbm.at[:, columns(mp_at(k))], w.at[mp_at(k)]) for k in range(n_mp)]
    t_copy = load(tgt_hbm, tgt)
    m_copy = load(m_hbm.at[0], mom1)
    v_copy = load(v_hbm.at[0], mom2)
    sends = []

    def go(copy):
        copy.start()
        sends.append(copy)

    low = (mp < n_mp // 2).astype(jnp.int32)

    def other_at(i):
        down = n_mp - 1 - i
        down = down - (down <= mp).astype(jnp.int32)
        up = i + (mp <= i).astype(jnp.int32)
        return low * down + (1 - low) * up

    order = list(reversed(range(n_mp - 1)))

    class Relay:
        def __init__(self, at, parts, send, recv):
            self.at, self.parts, self.send, self.recv = at, parts, send, recv
            self.hops = [(i, c) for c in range(parts) for i in order[:2]]
            self.hops += [(i, c) for i in order[2:] for c in range(parts)]

        def copy(self, j, lane, c, where):
            part = self.at(j, c)
            return remote(part, part, self.send.at[lane, c], self.recv.at[j, c], (dp, where))

        def own(self, act):
            for c in range(self.parts):
                for lane, (onward, to) in enumerate(((mp > 0, mp - 1), (mp < n_mp - 1, mp + 1))):
                    copy = self.copy(mp, lane, c, to)
                    pl.when(onward)(copy.start if act else copy.wait_send)

        def hop(self, i, c):
            j = other_at(i)
            below = (j > mp).astype(jnp.int32)
            to = mp + 1 - 2 * below
            onward = jnp.logical_and(to >= 0, to < n_mp)
            return onward, self.copy(j, 2 + i, c, to)

        def forward(self, hops):
            for i, c in hops:
                onward, copy = self.hop(i, c)
                copy.wait_recv()
                pl.when(onward)(copy.start)

        def pull(self, i):
            self.forward([(i, c) for c in range(self.parts)])

        def sent(self):
            self.own(False)
            for i, c in self.hops:
                onward, copy = self.hop(i, c)
                pl.when(onward)(copy.wait_send)

    half = toks // 2
    xs = Relay(lambda j, c: xbuf.at[j, c * half:(c + 1) * half], 2, x_send, x_recv)
    c_parts = 2 if chunk % 32 == 0 else 1
    c_size = chunk // c_parts
    cs = Relay(
        lambda j, c: cpad.at[j, pl.ds(pl.multiple_of(inside + c * c_size, c_size), c_size)],
        c_parts, c_send, c_recv,
    )

    def block(j, first):
        x = xbuf[j]
        for i in range(tiles):
            at = slice(i * tile, (i + 1) * tile)
            term = dot_nt(x, w[j, at, :])
            if first:
                y[:, at] = term
            else:
                y[:, at] += term
        term = jnp.dot(x, b[columns(j), :], preferred_element_type=F32)
        if first:
            r[...] = term
        else:
            r[...] += term

    def swap(s, c):
        return remote(
            send1.at[s, c], recv1.at[s, c], s1_send.at[s, c], s1_recv.at[s, c], (partner, mp)
        )

    def swap_start(s, chips):
        for c in chips:
            send1[s, c] = g[min(s, 1), owner_rows(c * 2 + 1 - core), :].astype(BF16)
            go(swap(s, c))

    def tile_chips(i):
        return range(i * per_tile, (i + 1) * per_tile)

    def scatter_copy(s, c, slot, where):
        return remote(
            send2.at[s, c], recv2.at[s, slot], s2_send.at[s, c], s2_recv.at[s, slot], (where, mp)
        )

    def scatter_start(s):
        for c in others:
            swap(s, c).wait_recv()
            total = g[min(s, 1), owner_rows(c * 2 + core), :] + recv1[s, c].astype(F32)
            send2[s, c] = total.astype(BF16)
            go(scatter_copy(s, c, chip, c * 2 + core))
        swap(s, chip).wait_recv()
        g[min(s, 1), owner_rows(dp), :] += recv1[s, chip].astype(F32)

    def scatter_finish(s):
        total = g[min(s, 1), owner_rows(dp), :]
        for c in reversed(others):
            scatter_copy(s, c, c, c * 2 + core).wait_recv()
            total = total + recv2[s, c].astype(F32)
        return total

    def adam(total):
        projected = total / total_tokens
        first = 0.9 * mom1[...] + 0.1 * projected
        second = 0.95 * mom2[...] + 0.05 * projected * projected
        mom1[...] = first
        mom2[...] = second
        return (-0.02) * (first / (jnp.sqrt(second) + 1e-08))

    def gather_copy(s, owner, sem_at, where):
        part = d_out.at[owner_rows(owner), :] if s else rall.at[block_at(owner, toks), :]
        return remote(part, part, d_send.at[s, sem_at], d_recv.at[s, owner], where)

    def gather_start(s):
        for c in reversed(others):
            go(gather_copy(s, dp, c, (c * 2 + core, mp)))
        go(gather_copy(s, dp, n_ch + chip, (partner, mp)))

    def gather_forward(s, chips):
        for c in chips:
            owner = c * 2 + core
            gather_copy(s, owner, c, (owner, mp)).wait_recv()
            go(gather_copy(s, owner, n_ch + c, (partner, mp)))

    def gathered(s, c):
        gather_copy(s, c * 2 + 1 - core, n_ch + c, (partner, mp)).wait_recv()

    def lift(first, at, count):
        both = pl.ds(pl.multiple_of(first * rows, rows), count * rows)
        put = pl.ds(pl.multiple_of(at * rows, rows), count * rows)
        for j in range(n_mp):
            cols = slice(j * fin, (j + 1) * fin)
            lifted = dot_nt(d_out[both, :], b[cols, :])
            w_out[put, cols] = (w[j, both, :].astype(F32) + lifted).astype(BF16)

    x1_copy.wait()
    b_copies[0].wait()
    rpart[...] = jnp.dot(x1[...], b[columns(mp), :], preferred_element_type=F32)
    for q in range(n_mp):
        zsend[q] = rpart[q * piece:(q + 1) * piece, :].astype(BF16)
    if window > chunk:
        cpad[...] = jnp.zeros_like(cpad)
    x0_copy.wait()
    pl.semaphore_wait(barrier, len(peers))

    def reduce_copy(q, slot, where):
        return remote(
            zsend.at[q], zrecv.at[slot], z_send.at[0, q], z_recv.at[0, slot], (dp, where)
        )

    def mine(q):
        at = dp * toks + q * piece
        return rall.at[pl.ds(pl.multiple_of(at, piece), piece), :]

    def spread_copy(q, lane, where):
        return remote(mine(q), mine(q), z_send.at[1, lane], z_recv.at[1, q], (dp, where))

    for k in range(1, n_mp):
        go(reduce_copy(other_at(k - 1), mp, other_at(k - 1)))
    total = rpart[block_at(mp, piece), :]
    for k in range(1, n_mp):
        q = mp_at(k)
        reduce_copy(q, q, q).wait_recv()
        total = total + zrecv[q].astype(F32)
    mine(mp)[...] = total.astype(BF16)
    for k in range(1, n_mp):
        go(spread_copy(mp, k, other_at(k - 1)))
    xs.own(True)

    def relay(way, first, last):
        ready = len(order[:2])
        cuts = [0, ready, ready * way.parts, len(way.hops)]
        pl.when(inner)(lambda: way.forward(way.hops[cuts[first]:cuts[last]]))

    for k in range(1, n_mp):
        q = mp_at(k)
        spread_copy(q, k, q).wait_recv()

    def reduced1():
        return rall[block_at(dp, toks), :]

    gather_start(0)
    for i in range(tiles):
        at = slice(i * tile, (i + 1) * tile)
        g[1, at, :] = dot_tn(x1[:, at], reduced1())
        swap_start(2, tile_chips(i))
    relay(xs, 0, 1)
    scatter_start(2)
    relay(xs, 1, 3)
    for copy in b_copies[1:]:
        copy.wait()
    for copy in w_copies:
        copy.wait()
    block(mp, True)
    for i in order[:-1]:
        pl.when(outer)(lambda i=i: xs.pull(i))
        block(other_at(i), False)
    total = scatter_finish(2)
    cpad[mp, pl.ds(pl.multiple_of(inside, chunk), chunk), :] = total.astype(BF16)
    cs.own(True)
    gather_forward(0, reversed(others))
    pl.when(outer)(lambda: xs.pull(order[-1]))
    block(other_at(order[-1]), False)
    t_copy.wait()
    reduced = r[...].astype(BF16)
    for i in range(tiles):
        at = slice(i * tile, (i + 1) * tile)
        outputs = y[:, at].astype(BF16).astype(F32)
        e = (outputs - tgt[0, :, at].astype(F32)).astype(BF16)
        g[0, at, :] = dot_tn(e, reduced)
        swap_start(0, tile_chips(i))

    def span(j, at):
        return jnp.dot(
            w[j, at, pl.ds(pl.multiple_of(start, window), window)], cpad[j],
            preferred_element_type=F32,
        )

    for i in range(tiles):
        at = slice(i * tile, (i + 1) * tile)
        g[1, at, :] = span(mp, at) - dot_tn(tgt[1, :, at], reduced1())
    relay(cs, 0, 2)
    scatter_start(0)
    relay(cs, 2, 3)
    for k in order[:-1]:
        pl.when(outer)(lambda k=k: cs.pull(k))
        for i in range(tiles):
            at = slice(i * tile, (i + 1) * tile)
            g[1, at, :] += span(other_at(k), at)
    pl.when(outer)(lambda: cs.pull(order[-1]))
    for c in others + [chip]:
        at = block_at(c, 2 * rows)
        g[1, at, :] += span(other_at(order[-1]), at)
        swap_start(1, [c])
    scatter_start(1)
    for c in range(n_ch):
        gathered(0, c)
    gram = dot_tn(rall[...], rall[...]).astype(BF16)
    m_copy.wait()
    v_copy.wait()
    d0[...] = adam(scatter_finish(0)).astype(BF16)
    corr[...] = jnp.dot(d0[...], gram, preferred_element_type=F32)
    step = adam(scatter_finish(1) + corr[...])
    d_out[owner_rows(dp), :] = (d0[...].astype(F32) + step).astype(BF16)
    gather_start(1)
    m_done = pltpu.make_async_copy(mom1, m_out.at[0], o_sem.at[0])
    v_done = pltpu.make_async_copy(mom2, v_out.at[0], o_sem.at[1])
    m_done.start()
    v_done.start()
    gathered(1, chip)
    lift(chip * 2, side * 2, 2)
    arrivals = list(reversed(others))
    gather_forward(1, arrivals[:-1])
    gathered(1, near)
    lift(near * 2, (1 - side) * 2, 2)
    gather_forward(1, arrivals[-1:])
    for c in others[:-1]:
        gathered(1, c)
    for copy in sends:
        copy.wait_send()
    xs.sent()
    cs.sent()
    m_done.wait()
    v_done.wait()


def last_lift(n_dp, width, w, mine, d, b, first, second, w_out, m_out, v_out, stage, sem, s_sem):
    out_rows, features = w.shape
    deep = mine.shape[0]
    n_pairs = out_rows // deep
    pair = lax.div(lax.axis_index("dp"), 4)

    def rows_of(q):
        return pl.ds(pl.multiple_of(q * deep, deep), deep)

    copies = [
        pltpu.make_async_copy(mine, w_out.at[rows_of(pair)], s_sem.at[0]),
        pltpu.make_async_copy(first, m_out, s_sem.at[1]),
        pltpu.make_async_copy(second, v_out, s_sem.at[2]),
    ]
    for copy in copies:
        copy.start()
    for k in range(1, n_pairs):
        rows = rows_of(lax.rem(pair + k, n_pairs))
        for i in range(features // width):
            at = slice(i * width, (i + 1) * width)
            lifted = dot_nt(d[rows, :], b[at, :])
            stage[k - 1, :, at] = (w[rows, at].astype(F32) + lifted).astype(BF16)
            copy = pltpu.make_async_copy(
                stage.at[k - 1, :, at], w_out.at[rows, at], sem.at[k - 1, i]
            )
            copy.start()
            copies.append(copy)
    for copy in copies:
        copy.wait()


def local(n_dp, n_mp, tokens, targets, weight, basis, moment1, moment2):
    steps, toks, fin = tokens.shape
    out_rows, features = weight.shape
    rank = basis.shape[1]
    rows = moment1.shape[1]
    n_ch = n_dp // 2
    hbm = pl.BlockSpec(memory_space=pltpu.HBM)
    vmem = pl.BlockSpec(memory_space=pltpu.VMEM)
    anywhere = pl.BlockSpec(memory_space=pl.ANY)
    dma = pltpu.SemaphoreType.DMA
    mine, d, first, second = pl.pallas_call(
        functools.partial(kernel, n_dp, n_mp, toks * n_dp),
        out_shape=(
            jax.ShapeDtypeStruct((4 * rows, features), BF16),
            jax.ShapeDtypeStruct((out_rows, rank), BF16),
            jax.ShapeDtypeStruct((1, rows, rank), F32),
            jax.ShapeDtypeStruct((1, rows, rank), F32),
        ),
        in_specs=[hbm] * 6,
        out_specs=(vmem, vmem, anywhere, anywhere),
        scratch_shapes=[
            pltpu.VMEM((n_mp, toks, fin), BF16),
            pltpu.VMEM((toks, fin), BF16),
            pltpu.VMEM((steps, toks, out_rows), BF16),
            pltpu.VMEM((n_mp, out_rows, fin), BF16),
            pltpu.VMEM((features, rank), BF16),
            pltpu.VMEM((rows, rank), F32),
            pltpu.VMEM((rows, rank), F32),
            pltpu.VMEM((toks, out_rows), F32),
            pltpu.VMEM((toks, rank), F32),
            pltpu.VMEM((2, out_rows, rank), F32),
            pltpu.VMEM((3, n_ch, rows, rank), BF16),
            pltpu.VMEM((3, n_ch, rows, rank), BF16),
            pltpu.VMEM((3, n_ch, rows, rank), BF16),
            pltpu.VMEM((3, n_ch, rows, rank), BF16),
            pltpu.VMEM((n_dp * toks, rank), BF16),
            pltpu.VMEM((toks, rank), F32),
            pltpu.VMEM((n_mp, toks // n_mp, rank), BF16),
            pltpu.VMEM((n_mp, toks // n_mp, rank), BF16),
            pltpu.VMEM((n_mp, max(128, fin // n_dp), rank), BF16),
            pltpu.VMEM((rows, rank), BF16),
            pltpu.VMEM((rows, rank), F32),
            dma((2 * n_mp + 5,)),
            dma((n_mp + 1, 2)),
            dma((n_mp, 2)),
            dma((n_mp + 1, 2)),
            dma((n_mp, 2)),
            dma((2, n_mp)),
            dma((2, n_mp)),
            dma((3, n_ch)),
            dma((3, n_ch)),
            dma((3, n_ch)),
            dma((3, n_ch)),
            dma((2, n_dp)),
            dma((2, n_dp)),
            dma((2,)),
        ],
        compiler_params=pltpu.CompilerParams(
            collective_id=0, has_side_effects=True, vmem_limit_bytes=38 * 2**20
        ),
    )(*[
        pltpu.with_memory_space_constraint(x, pltpu.HBM)
        for x in (tokens, targets, weight, basis, moment1, moment2)
    ])
    width = min(512, features)
    return pl.pallas_call(
        functools.partial(last_lift, n_dp, width),
        out_shape=(
            jax.ShapeDtypeStruct((out_rows, features), BF16),
            jax.ShapeDtypeStruct((1, rows, rank), F32),
            jax.ShapeDtypeStruct((1, rows, rank), F32),
        ),
        in_specs=[vmem] * 6,
        out_specs=(hbm,) * 3,
        scratch_shapes=[
            pltpu.VMEM((n_ch // 2 - 1, 4 * rows, features), BF16),
            dma((n_ch // 2 - 1, features // width)),
            dma((3,)),
        ],
        compiler_params=pltpu.CompilerParams(vmem_limit_bytes=12 * 2**20),
    )(weight, mine, d, basis, first, second)


def solution(mesh):
    in_specs = (
        P(None, "dp", "mp"),
        P(None, "dp", "mp"),
        P("mp", None),
        P(),
        P("mp", "dp", None),
        P("mp", "dp", None),
    )
    out_specs = (P("mp", None), P("mp", "dp", None), P("mp", "dp", None))
    body = functools.partial(local, mesh.shape["dp"], mesh.shape["mp"])
    return jax.shard_map(body, mesh=mesh, in_specs=in_specs, out_specs=out_specs, check_vma=False)
```
